32 devices in a mesh: grp: 2 (over x), inp: 4 (over y, core), out: 4 (over z).
Axes of the slice: x: 2, y: 2, z: 4, core: 2. Of those that a mesh axis runs over, the one named last changes fastest.
Arguments:
- activations: bfloat16 [4, 512, 8192], P('grp', 'out', 'inp'), parts along dimension 0, may hold values from -6 to 6
- out_grads: bfloat16 [4, 512, 28672], P('grp', 'inp', 'out'), parts along dimension 0, may hold values from -6 to 6
- query_grads: bfloat16 [2, 28672, 8192], P(None, 'out', 'inp'), may hold values from -0.00036621094 to 0.00036621094
- token_ids: int32 [4, 512], P('grp'), parts along dimension 0, may hold values from 0 to 128255
- loss_mask: int32 [4, 512], P('grp'), parts along dimension 0, may hold values 0 or 1
Outputs:
- scores: float32 [2, 4, 512], P(None, 'grp'), parts along dimension 1
The draws below stay inside these ranges and needn't reach their ends.
There are 2 independent parts, one for each index of `grp`. The reference program is written for one: setup_inputs(seed, part) draws one part's arguments, and reference() takes and returns one part's arrays. A program takes and returns all parts, laid end to end along the dimension named above; an argument that names none is the same for every part. Nothing has to cross between parts.
All inputs are finite; a program needn't handle non-finite values.
Results may differ from the reference program's by a relative error of at most 0.0003.
Values may be sent and summed in bfloat16 or wider, within the bound.
A program may use at most 128 MiB of HBM per device.

```python
import math
import jax
import jax.numpy as jnp
import numpy as np

D = 8192
FF = 28672
VOCAB = 128256
NQ = 2
BLOCK_TOK = 512
BLOCKS = 2


def set_ends(drawn, rng, smallest, top_value):
    spot = [jax.random.randint(jax.random.fold_in(rng, axis), (), 0, length) for axis, length in enumerate(drawn.shape)]
    main_axis = drawn.shape.index(max(drawn.shape))
    beside = spot[:main_axis] + [(spot[main_axis] + 1) % drawn.shape[main_axis]] + spot[main_axis + 1:]
    return drawn.at[tuple(spot)].set(smallest).at[tuple(beside)].set(top_value)


def level_of(key, shape, shards, low, top_value):
    loudness = 1.0
    for axis_at, parts in shards:
        steps = jax.random.uniform(jax.random.fold_in(jax.random.fold_in(key, 6), axis_at), (parts,), jnp.float32, low / len(shards), top_value / len(shards))
        loudness = loudness * jnp.repeat(jnp.exp(steps), shape[axis_at] // parts).reshape((-1,) + (1,) * (len(shape) - 1 - axis_at))
    return loudness


def wide_ids(stream_key, shape, number_of, lean):
    portions = [min(1 << octave, number_of + 1 - (1 << octave)) * (1 << 20) // math.isqrt((1 << octave) ** lean) + 1 for octave in range((number_of + 1).bit_length()) if 1 << octave <= number_of]
    scale = 1 + sum(portions) // (1 << 30)
    grid = np.cumsum(np.array([max(1, weight // scale) for weight in portions]))
    lot = jax.random.randint(jax.random.fold_in(stream_key, 1), shape, 0, int(grid[len(portions) - 1]))
    start = jnp.left_shift(1, jnp.searchsorted(jnp.asarray(grid, jnp.int32), lot, side="right").astype(jnp.int32))
    grade = start - 1 + jax.random.randint(jax.random.fold_in(stream_key, 4), shape, 0, 1 << 30) % jnp.minimum(start, number_of + 1 - start)
    return jax.random.permutation(jax.random.fold_in(stream_key, 2), number_of)[grade].astype(jnp.int32)


def scatter_about(own_key, shape, width, most, cuts=(), kind=jnp.bfloat16):
    result = width * jax.random.normal(own_key, shape, jnp.float32)
    if cuts:
        result = result * level_of(own_key, shape, cuts, -0.22, 0.18)
    return jnp.clip(result, -most, most).astype(kind)


def setup_inputs(seed: int = 0, part: int = 0) -> dict:
    splits = jax.random.split(jax.random.key(seed), 6)
    own_keys = jax.random.split(jax.random.fold_in(splits[5], part), 6)
    activations = scatter_about(own_keys[0], (BLOCKS, BLOCK_TOK, D), 1.0, 6.0, ((1, 4), (2, 4)))
    out_grads = scatter_about(own_keys[1], (BLOCKS, BLOCK_TOK, FF), 1.0, 6.0, ((1, 4), (2, 4)))
    query_grads = scatter_about(splits[2], (NQ, FF, D), (FF * D) ** -0.5, 0.00036621094, ((1, 4), (2, 4)))
    token_ids = set_ends(wide_ids(own_keys[3], (BLOCKS, BLOCK_TOK), VOCAB, 2), jax.random.fold_in(own_keys[3], 3), 0, VOCAB - 1).astype(jnp.int32)
    loss_mask = set_ends((jax.random.randint(own_keys[4], (BLOCKS, BLOCK_TOK), 0, 4) < 3).astype(jnp.int32), jax.random.fold_in(own_keys[4], 1), 0, 1)
    return {"activations": activations, "out_grads": out_grads, "query_grads": query_grads, "token_ids": token_ids, "loss_mask": loss_mask}


def reference(activations, out_grads, query_grads, token_ids, loss_mask):
    equal = token_ids[:, :, None] == token_ids[:, None, :]
    counts = jnp.sum(equal.astype(jnp.int32), axis=2)
    weight = loss_mask.astype(jnp.float32) / counts.astype(jnp.float32)
    per_block = []
    for number in range(BLOCKS):
        per_query = []
        for query in range(NQ):
            projected = jnp.dot(out_grads[number], query_grads[query], preferred_element_type=jnp.float32)
            per_query.append(jnp.sum(projected * activations[number].astype(jnp.float32), axis=1))
        per_block.append(jnp.stack(per_query, axis=1))
    raw = jnp.stack(per_block)
    return jnp.transpose(raw * weight[:, :, None], (2, 0, 1))
```

```python
import functools

import jax
import jax.numpy as jnp
from jax import lax
from jax.experimental import pallas as pl
from jax.experimental.pallas import tpu as pltpu
from jax.sharding import PartitionSpec as P

MESH = pl.DeviceIdType.MESH


def score_kernel(n_inp, n_out, chunk, width, g_ref, a_ref, q_ref, r_ref, gbuf, abuf, acc, qbuf, xin, xout,
                 own_sem, gsend, grecv, psend, precv, asend, arecv, qsem, isend, irecv, osend, orecv):
    chips = n_inp // 2
    me, z = lax.axis_index("inp"), lax.axis_index("out")
    y, core = me // 2, lax.rem(me, 2)
    partner = y * 2 + 1 - core
    nq, _, cols = q_ref.shape
    nb, tsh, feats = g_ref.shape
    atok = a_ref.shape[1]
    chunks = feats // chunk
    total = chips * chunks
    slots = qbuf.shape[0]
    rows = 2 * nb * tsh

    def remote(src, dst, send, recv, **where):
        return pltpu.make_async_remote_copy(
            src_ref=src, dst_ref=dst, send_sem=send, recv_sem=recv, device_id=where, device_id_type=MESH)

    def part_of(c):
        return g_ref.at[:, :, pl.ds(pl.multiple_of(c * chunk, chunk), chunk)]

    def own_copy(c):
        return pltpu.make_async_copy(part_of(c), gbuf.at[c, 0, core], own_sem.at[c])

    def far_copy(d, c):
        return remote(part_of(c), gbuf.at[c, d, core], gsend.at[d - 1, c], grecv.at[d - 1, c],
                      inp=lax.rem(y + chips - d, chips) * 2 + core)

    def near_copy(c):
        return remote(part_of(c), gbuf.at[c, 0, core], psend.at[0, c], precv.at[0, c], inp=partner)

    def pass_on(d, c):
        return remote(gbuf.at[c, d, core], gbuf.at[c, d, core], psend.at[d, c], precv.at[d, c], inp=partner)

    def rows_of(at):
        return pl.ds(pl.multiple_of(at * atok, atok), atok)

    def ring_copy(k):
        owner = lax.rem(z + n_out - (k - 1), n_out)
        src = a_ref if k == 1 else abuf.at[:, rows_of(owner), :]
        return remote(src, abuf.at[:, rows_of(owner), :], asend.at[k - 1], arecv.at[k - 1], out=lax.rem(z + 1, n_out))

    def q_copy(step):
        g, q = step // nq, lax.rem(step, nq)
        c = lax.rem(g, chunks)
        slot = lax.rem(step, slots)
        return pltpu.make_async_copy(
            q_ref.at[q, pl.ds(pl.multiple_of(c * chunk, chunk), chunk), :], qbuf.at[slot], qsem.at[slot])

    a_own = pltpu.make_async_copy(a_ref, abuf.at[:, rows_of(z), :], own_sem.at[chunks])
    a_own.start()
    for step in range(slots - 1):
        q_copy(jnp.int32(step)).start()
    for c in range(chunks):
        own_copy(c).start()

    barrier = pltpu.get_barrier_semaphore()
    for d in range(1, n_inp):
        pl.semaphore_signal(barrier, inc=1, device_id={"inp": lax.rem(me + d, n_inp)}, device_id_type=MESH)
    for d in range(1, n_out):
        pl.semaphore_signal(barrier, inc=1, device_id={"out": lax.rem(z + d, n_out)}, device_id_type=MESH)
    pl.semaphore_wait(barrier, n_inp + n_out - 2)

    for d in range(1, chips):
        for c in range(chunks):
            far_copy(d, c).start()
    ring_copy(1).start()
    for c in range(chunks):
        near_copy(c).start()

    def zero(i, _):
        acc[i // nq, lax.rem(i, nq)] = jnp.zeros((rows, cols), jnp.float32)
        return 0

    lax.fori_loop(0, chips * nq, zero, 0)

    def advance(g, _):
        p, c = g // chunks, lax.rem(g, chunks)

        @pl.when(p == 0)
        def _():
            own_copy(c).wait()
            near_copy(c).wait_recv()

        @pl.when(p > 0)
        def _():
            far_copy(p, c).wait_recv()
            pass_on(p, c).start()
            pass_on(p, c).wait_recv()

        for q in range(nq):
            step = g * nq + q

            @pl.when(step + slots - 1 < total * nq)
            def _():
                q_copy(step + slots - 1).start()

            q_copy(step).wait()
            slot = lax.rem(step, slots)

            def tile(n, _):
                at = pl.ds(pl.multiple_of(n * width, width), width)
                left = gbuf[c, p].reshape(rows, chunk)
                acc[p, q, :, at] += jnp.dot(left, qbuf[slot, :, at], preferred_element_type=jnp.float32)
                return 0

            lax.fori_loop(0, cols // width, tile, 0)
        return 0

    def finish(p, _):
        for k in range(2):
            shard = lax.rem(y + p, chips) * 2 + k
            for b in range(nb):
                act = abuf.at[b, pl.ds(pl.multiple_of(shard * tsh, tsh), tsh), :]
                top = (k * nb + b) * tsh
                for q in range(nq):
                    fold = jnp.zeros((tsh, 128), jnp.float32)
                    for n in range(cols // 128):
                        at = slice(n * 128, (n + 1) * 128)
                        fold += acc[p, q, top:top + tsh, at] * act[:, at].astype(jnp.float32)
                    xin[me, shard, q * nb + b, :] = jnp.sum(fold.T, axis=0)
        return 0

    at = 0
    for k in range(2, n_out):
        stop = min((k - 1) * 5, total - 1)
        lax.fori_loop(at, stop, advance, 0)
        at = stop
        ring_copy(k - 1).wait_recv()
        ring_copy(k).start()
    lax.fori_loop(at, total - 1, advance, 0)
    a_own.wait()
    if n_out > 1:
        ring_copy(n_out - 1).wait_recv()
    lax.fori_loop(0, chips - 1, finish, 0)
    lax.fori_loop(total - 1, total, advance, 0)
    finish(jnp.int32(chips - 1), 0)

    def in_copy(d):
        return remote(xin.at[me], xin.at[me], isend.at[d - 1], irecv.at[d - 1], inp=lax.rem(me + d, n_inp))

    def out_copy(d):
        return remote(xout.at[z], xout.at[z], osend.at[d - 1], orecv.at[d - 1], out=lax.rem(z + d, n_out))

    for d in range(1, n_inp):
        in_copy(d).start()
    for d in range(1, n_inp):
        in_copy(d).wait_recv()
    value = xin[0]
    for i in range(1, n_inp):
        value += xin[i]
    xout[z] = value
    for d in range(1, n_out):
        out_copy(d).start()
    for d in range(1, n_out):
        out_copy(d).wait_recv()
    value = xout[0]
    for i in range(1, n_out):
        value += xout[i]
    r_ref[...] = value

    for c in range(chunks):
        near_copy(c).wait_send()
        for d in range(1, chips):
            far_copy(d, c).wait_send()
            pass_on(d, c).wait_send()
    for k in range(1, n_out):
        ring_copy(k).wait_send()
        out_copy(k).wait_send()
    for d in range(1, n_inp):
        in_copy(d).wait_send()


def shards(n_inp, n_out, activations, out_grads, query_grads, token_ids, loss_mask):
    nb, tsh, feats = out_grads.shape
    nq, _, cols = query_grads.shape
    tokens = token_ids.shape[1]
    chips = n_inp // 2
    chunk = next(size for size in (1024, 512, 256, 128) if feats % size == 0)
    width = next(size for size in (512, 256, 128) if cols % size == 0)
    chunks = feats // chunk
    dma = pltpu.SemaphoreType.DMA
    raw = pl.pallas_call(
        functools.partial(score_kernel, n_inp, n_out, chunk, width),
        out_shape=jax.ShapeDtypeStruct((n_inp, nq * nb, tsh), jnp.float32),
        in_specs=[pl.BlockSpec(memory_space=pl.ANY)] * 3,
        out_specs=pl.BlockSpec(memory_space=pltpu.VMEM),
        scratch_shapes=[
            pltpu.VMEM((chunks, chips, 2, nb, tsh, chunk), jnp.bfloat16),
            pltpu.VMEM((nb, tokens, cols), jnp.bfloat16),
            pltpu.VMEM((chips, nq, 2 * nb * tsh, cols), jnp.float32),
            pltpu.VMEM((3, chunk, cols), jnp.bfloat16),
            pltpu.VMEM((n_inp, n_inp, nq * nb, tsh), jnp.float32),
            pltpu.VMEM((n_out, n_inp, nq * nb, tsh), jnp.float32),
            dma((chunks + 1,)),
            dma((max(chips - 1, 1), chunks)),
            dma((max(chips - 1, 1), chunks)),
            dma((chips, chunks)),
            dma((chips, chunks)),
            dma((max(n_out - 1, 1),)),
            dma((max(n_out - 1, 1),)),
            dma((3,)),
            dma((max(n_inp - 1, 1),)),
            dma((max(n_inp - 1, 1),)),
            dma((max(n_out - 1, 1),)),
            dma((max(n_out - 1, 1),)),
        ],
        compiler_params=pltpu.CompilerParams(
            collective_id=0, has_side_effects=True, vmem_limit_bytes=63 * 1024 * 1024),
    )(out_grads, activations, query_grads)
    equal = token_ids[:, :, None] == token_ids[:, None, :]
    counts = jnp.sum(equal.astype(jnp.int32), axis=2)
    weight = loss_mask.astype(jnp.float32) / counts.astype(jnp.float32)
    raw = jnp.transpose(raw.reshape(n_inp, nq, nb, tsh), (1, 2, 0, 3)).reshape(nq, nb, tokens)
    return raw * weight[None]


def solution(mesh):
    in_specs = (
        P("grp", "out", "inp"),
        P("grp", "inp", "out"),
        P(None, "out", "inp"),
        P("grp", None),
        P("grp", None),
    )
    body = functools.partial(shards, mesh.shape["inp"], mesh.shape["out"])
    return jax.shard_map(body, mesh=mesh, in_specs=in_specs, out_specs=P(None, "grp", None), check_vma=False)
```

```python
import functools

import jax
import jax.numpy as jnp
from jax import lax
from jax.experimental import pallas as pl
from jax.experimental.pallas import tpu as pltpu
from jax.sharding import PartitionSpec as P

MESH = pl.DeviceIdType.MESH


def score_kernel(n_inp, n_out, chunk, width, g_ref, a_ref, q_ref, r_ref, gbuf, abuf, acc, qbuf, xin, xout,
                 own_sem, gsend, grecv, psend, precv, asend, arecv, qsem, isend, irecv, osend, orecv):
    chips = n_inp // 2
    me, z = lax.axis_index("inp"), lax.axis_index("out")
    y, core = me // 2, lax.rem(me, 2)
    partner = y * 2 + 1 - core
    nq, _, cols = q_ref.shape
    nb, tsh, feats = g_ref.shape
    atok = a_ref.shape[1]
    chunks = feats // chunk
    total = chips * chunks
    slots = qbuf.shape[0]
    rows = 2 * nb * tsh

    def remote(src, dst, send, recv, **where):
        return pltpu.make_async_remote_copy(
            src_ref=src, dst_ref=dst, send_sem=send, recv_sem=recv, device_id=where, device_id_type=MESH)

    def part_of(c):
        return g_ref.at[:, :, pl.ds(pl.multiple_of(c * chunk, chunk), chunk)]

    def own_copy(c):
        return pltpu.make_async_copy(part_of(c), gbuf.at[c, 0, core], own_sem.at[c])

    def far_copy(d, c):
        return remote(part_of(c), gbuf.at[c, d, core], gsend.at[d - 1, c], grecv.at[d - 1, c],
                      inp=lax.rem(y + chips - d, chips) * 2 + core)

    def near_copy(c):
        return remote(part_of(c), gbuf.at[c, 0, core], psend.at[0, c], precv.at[0, c], inp=partner)

    def pass_on(d, c):
        return remote(gbuf.at[c, d, core], gbuf.at[c, d, core], psend.at[d, c], precv.at[d, c], inp=partner)

    def rows_of(at):
        return pl.ds(pl.multiple_of(at * atok, atok), atok)

    def ring_copy(k):
        owner = lax.rem(z + n_out - (k - 1), n_out)
        src = a_ref if k == 1 else abuf.at[:, rows_of(owner), :]
        return remote(src, abuf.at[:, rows_of(owner), :], asend.at[k - 1], arecv.at[k - 1], out=lax.rem(z + 1, n_out))

    def q_copy(step):
        g, q = step // nq, lax.rem(step, nq)
        c = lax.rem(g, chunks)
        slot = lax.rem(step, slots)
        return pltpu.make_async_copy(
            q_ref.at[q, pl.ds(pl.multiple_of(c * chunk, chunk), chunk), :], qbuf.at[slot], qsem.at[slot])

    a_own = pltpu.make_async_copy(a_ref, abuf.at[:, rows_of(z), :], own_sem.at[chunks])
    a_own.start()
    for step in range(slots - 1):
        q_copy(jnp.int32(step)).start()
    for c in range(chunks):
        own_copy(c).start()

    barrier = pltpu.get_barrier_semaphore()
    for d in range(1, n_inp):
        pl.semaphore_signal(barrier, inc=1, device_id={"inp": lax.rem(me + d, n_inp)}, device_id_type=MESH)
    for d in range(1, n_out):
        pl.semaphore_signal(barrier, inc=1, device_id={"out": lax.rem(z + d, n_out)}, device_id_type=MESH)
    pl.semaphore_wait(barrier, n_inp + n_out - 2)

    for d in range(1, chips):
        for c in range(chunks):
            far_copy(d, c).start()
    ring_copy(1).start()
    for c in range(chunks):
        near_copy(c).start()

    def zero(i, _):
        acc[i // nq, lax.rem(i, nq)] = jnp.zeros((rows, cols), jnp.float32)
        return 0

    lax.fori_loop(0, chips * nq, zero, 0)

    def multiply(g, load, keep):
        p, c = g // chunks, lax.rem(g, chunks)
        for q in range(nq):
            step = g * nq + q

            if load:
                @pl.when(step + slots - 1 < total * nq)
                def _():
                    q_copy(step + slots - 1).start()

                q_copy(step).wait()
            slot = lax.rem(step, slots)

            def tile(n, _):
                at = pl.ds(pl.multiple_of(n * width, width), width)
                if keep is None:
                    left = gbuf[c, p].reshape(rows, chunk)
                    acc[p, q, :, at] += jnp.dot(left, qbuf[slot, :, at], preferred_element_type=jnp.float32)
                else:
                    half = pl.ds(pl.multiple_of(keep * (rows // 2), rows // 2), rows // 2)
                    left = gbuf[c, p, keep].reshape(rows // 2, chunk)
                    acc[p, q, half, at] += jnp.dot(left, qbuf[slot, :, at], preferred_element_type=jnp.float32)
                return 0

            lax.fori_loop(0, cols // width, tile, 0)

            if load and q == 0:
                @pl.when(jnp.logical_and(g + 1 >= chunks, g + 1 < total - 1))
                def _():
                    p_next, c_next = (g + 1) // chunks, lax.rem(g + 1, chunks)
                    far_copy(p_next, c_next).wait_recv()
                    pass_on(p_next, c_next).start()

    def advance(g, _):
        p, c = g // chunks, lax.rem(g, chunks)

        @pl.when(p == 0)
        def _():
            own_copy(c).wait()
            near_copy(c).wait_recv()

        @pl.when(p > 0)
        def _():
            pass_on(p, c).wait_recv()

        multiply(g, True, None)
        return 0

    def last_chunk():
        p, c = chips - 1, chunks - 1
        g = jnp.int32(total - 1)
        if p == 0:
            own_copy(c).wait()
            near_copy(c).wait_recv()
            multiply(g, True, None)
        else:
            far_copy(p, c).wait_recv()
            pass_on(p, c).start()
            multiply(g, True, core)
            pass_on(p, c).wait_recv()
            multiply(g, False, 1 - core)

    def finish(p, _):
        for k in range(2):
            shard = lax.rem(y + p, chips) * 2 + k
            for b in range(nb):
                act = abuf.at[b, pl.ds(pl.multiple_of(shard * tsh, tsh), tsh), :]
                top = (k * nb + b) * tsh
                for q in range(nq):
                    fold = jnp.zeros((tsh, 128), jnp.float32)
                    for n in range(cols // 128):
                        at = slice(n * 128, (n + 1) * 128)
                        fold += acc[p, q, top:top + tsh, at] * act[:, at].astype(jnp.float32)
                    xin[me, shard, q * nb + b, :] = jnp.sum(fold.T, axis=0)
        return 0

    at = 0
    for k in range(2, n_out):
        stop = min((k - 1) * 5, total - 1)
        lax.fori_loop(at, stop, advance, 0)
        at = stop
        ring_copy(k - 1).wait_recv()
        ring_copy(k).start()
    lax.fori_loop(at, total - 1, advance, 0)
    a_own.wait()
    if n_out > 1:
        ring_copy(n_out - 1).wait_recv()
    lax.fori_loop(0, chips - 1, finish, 0)
    last_chunk()
    finish(jnp.int32(chips - 1), 0)

    def in_copy(d):
        return remote(xin.at[me], xin.at[me], isend.at[d - 1], irecv.at[d - 1], inp=lax.rem(me + d, n_inp))

    def out_copy(d):
        return remote(xout.at[z], xout.at[z], osend.at[d - 1], orecv.at[d - 1], out=lax.rem(z + d, n_out))

    for d in range(1, n_inp):
        in_copy(d).start()
    for d in range(1, n_inp):
        in_copy(d).wait_recv()
    value = xin[0]
    for i in range(1, n_inp):
        value += xin[i]
    xout[z] = value
    for d in range(1, n_out):
        out_copy(d).start()
    for d in range(1, n_out):
        out_copy(d).wait_recv()
    value = xout[0]
    for i in range(1, n_out):
        value += xout[i]
    r_ref[...] = value

    for c in range(chunks):
        near_copy(c).wait_send()
        for d in range(1, chips):
            far_copy(d, c).wait_send()
            pass_on(d, c).wait_send()
    for k in range(1, n_out):
        ring_copy(k).wait_send()
        out_copy(k).wait_send()
    for d in range(1, n_inp):
        in_copy(d).wait_send()


def shards(n_inp, n_out, activations, out_grads, query_grads, token_ids, loss_mask):
    nb, tsh, feats = out_grads.shape
    nq, _, cols = query_grads.shape
    tokens = token_ids.shape[1]
    chips = n_inp // 2
    chunk = next(size for size in (1024, 512, 256, 128) if feats % size == 0)
    width = next(size for size in (2048, 1024, 512, 256, 128) if cols % size == 0)
    chunks = feats // chunk
    dma = pltpu.SemaphoreType.DMA
    raw = pl.pallas_call(
        functools.partial(score_kernel, n_inp, n_out, chunk, width),
        out_shape=jax.ShapeDtypeStruct((n_inp, nq * nb, tsh), jnp.float32),
        in_specs=[pl.BlockSpec(memory_space=pl.ANY)] * 3,
        out_specs=pl.BlockSpec(memory_space=pltpu.VMEM),
        scratch_shapes=[
            pltpu.VMEM((chunks, chips, 2, nb, tsh, chunk), jnp.bfloat16),
            pltpu.VMEM((nb, tokens, cols), jnp.bfloat16),
            pltpu.VMEM((chips, nq, 2 * nb * tsh, cols), jnp.float32),
            pltpu.VMEM((3, chunk, cols), jnp.bfloat16),
            pltpu.VMEM((n_inp, n_inp, nq * nb, tsh), jnp.float32),
            pltpu.VMEM((n_out, n_inp, nq * nb, tsh), jnp.float32),
            dma((chunks + 1,)),
            dma((max(chips - 1, 1), chunks)),
            dma((max(chips - 1, 1), chunks)),
            dma((chips, chunks)),
            dma((chips, chunks)),
            dma((max(n_out - 1, 1),)),
            dma((max(n_out - 1, 1),)),
            dma((3,)),
            dma((max(n_inp - 1, 1),)),
            dma((max(n_inp - 1, 1),)),
            dma((max(n_out - 1, 1),)),
            dma((max(n_out - 1, 1),)),
        ],
        compiler_params=pltpu.CompilerParams(
            collective_id=0, has_side_effects=True, vmem_limit_bytes=63 * 1024 * 1024),
    )(out_grads, activations, query_grads)
    equal = token_ids[:, :, None] == token_ids[:, None, :]
    counts = jnp.sum(equal.astype(jnp.int32), axis=2)
    weight = loss_mask.astype(jnp.float32) / counts.astype(jnp.float32)
    raw = jnp.transpose(raw.reshape(n_inp, nq, nb, tsh), (1, 2, 0, 3)).reshape(nq, nb, tokens)
    return raw * weight[None]


def solution(mesh):
    in_specs = (
        P("grp", "out", "inp"),
        P("grp", "inp", "out"),
        P(None, "out", "inp"),
        P("grp", None),
        P("grp", None),
    )
    body = functools.partial(shards, mesh.shape["inp"], mesh.shape["out"])
    return jax.shard_map(body, mesh=mesh, in_specs=in_specs, out_specs=P(None, "grp", None), check_vma=False)
```
